32 devices in a mesh: row: 8 (over z, x), col: 4 (over y, core).
Axes of the slice: x: 2, y: 2, z: 4, core: 2. Of those that a mesh axis runs over, the one named last changes fastest.
Arguments:
- positions: float32 [3, 8192], P(None, ('row', 'col')), may hold values from -6 to 6
- features: bfloat16 [128, 8192], P(None, ('row', 'col')), may hold values from -6 to 6
- fill: int32 [64], P(('row', 'col')), may hold values from 64 to 128, as said below
- tiles: int32 [256, 2], P(('row', 'col')), may hold values from 0 to 15, as said below
- tile_count: int32 [32], P(('row', 'col')), may hold values from 2 to 8, as said below
- w_radial: float32 [64, 32], replicated, may hold values from -1 to 1
- w_left: bfloat16 [128, 64], replicated, may hold values from -0.5 to 0.5
- w_right: bfloat16 [128, 64], replicated, may hold values from -0.5 to 0.5
- w_hidden: bfloat16 [64, 64], replicated, may hold values from -0.75 to 0.75
- w_out: bfloat16 [64], replicated, may hold values from -0.25 to 0.25
Outputs:
- forces: float32 [3, 8192], P(None, ('row', 'col'))
- bead_energy: float32 [8192], P(('row', 'col'))
The draws below stay inside these ranges and needn't reach their ends.
Inputs may be any that keep to these rules, and one draw needn't show every extreme that they name: `fill`: at least 64; some cluster holds 128. `tiles`: A device's 8 slots name distinct cluster pairs; the first entry is below 8, the second below 16; some device has the pair of the last clusters of both groups. `tile_count`: at least 2; some device has all 8 slots live.
All inputs are finite; a program needn't handle non-finite values.
Results may differ from the reference program's by a relative error of at most 0.0045.
Values may be sent and summed in bfloat16 or wider, within the bound.
A program may use at most 64 MiB of HBM per device.

```python
import jax
import jax.numpy as jnp
from jax import lax

CL = 128
HID = 64
EMB = 128
NRBF = 32
CPD = 2
MAXT = 8
NC = 64
NB = 8192
GR = 8
GC = 16
NTILES = 256
N_COL = 4


def draw_fill(key, part):
    counts = jax.random.randint(jax.random.fold_in(key, 11), (NC,), CL // 2, CL + 1)
    where = jax.random.randint(jax.random.fold_in(key, 12), (), 0, NC)
    return counts.at[where].set(CL).astype(jnp.int32)


def draw_tiles(key, part):
    devices = NTILES // MAXT
    chosen = jax.random.randint(jax.random.fold_in(key, 22), (), 0, devices)
    corner = GR * GC - 1

    def one(index):
        order = jax.random.permutation(jax.random.fold_in(jax.random.fold_in(key, 21), index), GR * GC)[:MAXT]
        present = jnp.any(order == corner)
        forced = jnp.where(present, order, order.at[0].set(corner))
        order = jnp.where(index == chosen, forced, order)
        return jnp.stack([order // GC, order % GC], 1)
    return jax.vmap(one)(jnp.arange(devices)).reshape(NTILES, 2).astype(jnp.int32)


def draw_tile_count(key, part):
    devices = NTILES // MAXT
    counts = jax.random.randint(jax.random.fold_in(key, 31), (devices,), 2, MAXT + 1)
    where = jax.random.randint(jax.random.fold_in(key, 32), (), 0, devices)
    return counts.at[where].set(MAXT).astype(jnp.int32)


def steps_of(own_key, dims, shards, least, largest):
    level = 1.0
    for position, parts in shards:
        heights = jax.random.uniform(jax.random.fold_in(jax.random.fold_in(own_key, 6), position), (parts,), jnp.float32, least / len(shards), largest / len(shards))
        level = level * jnp.repeat(jnp.exp(heights), dims[position] // parts).reshape((-1,) + (1,) * (len(dims) - 1 - position))
    return level


def gaussian(rng, extent, deviation, limit, cuts=(), kind=jnp.bfloat16):
    level = steps_of(rng, extent, cuts, -0.22, 0.18) if cuts else 1.0
    drawn = jax.random.normal(rng, extent, jnp.float32) * deviation * level
    return jnp.minimum(jnp.maximum(drawn, -limit), limit).astype(kind)


def setup_inputs(seed: int = 0) -> dict:
    streams_of = jax.random.split(jax.random.key(seed), 11)
    positions = gaussian(streams_of[0], (3, NB), 1.0, 6.0, ((1, 32),), jnp.float32)
    features = gaussian(streams_of[1], (EMB, NB), 1.0, 6.0, ((1, 32),))
    fill = draw_fill(jax.random.fold_in(streams_of[10], 71), 0)
    tiles = draw_tiles(jax.random.fold_in(streams_of[10], 71), 0)
    tile_count = draw_tile_count(jax.random.fold_in(streams_of[10], 71), 0)
    w_radial = gaussian(streams_of[5], (HID, NRBF), NRBF ** -0.5, 1.0, (), jnp.float32)
    w_left = gaussian(streams_of[6], (EMB, HID), EMB ** -0.5, 0.5)
    w_right = gaussian(streams_of[7], (EMB, HID), EMB ** -0.5, 0.5)
    w_hidden = gaussian(streams_of[8], (HID, HID), HID ** -0.5, 0.75)
    w_out = gaussian(streams_of[9], (HID,), (HID * 8) ** -0.5, 0.25)
    return dict(positions=positions, features=features, fill=fill, tiles=tiles, tile_count=tile_count, w_radial=w_radial, w_left=w_left, w_right=w_right, w_hidden=w_hidden, w_out=w_out)


SOFT = 0.01
RANGE = 6.0

def dsilu(value):
    sig = jax.nn.sigmoid(value)
    return sig * (1.0 + value * (1.0 - sig))

def tile_terms(left, right, proj_a, proj_b, same, live_tile, w_radial, w_hidden, w_out):
    slots = left.shape[1]
    hidden = w_radial.shape[0]
    nbasis = w_radial.shape[1]
    delta = left[:3, :, None] - right[:3, None, :]
    dist = jnp.sqrt(lax.optimization_barrier(jnp.sum(delta * delta, 0)) + SOFT)
    ident = (jnp.arange(slots)[:, None] == jnp.arange(slots)[None, :]).astype(jnp.float32)
    mask = left[3][:, None] * right[3][None, :] * (1.0 - same * ident) * live_tile
    flat = dist.reshape(-1)
    centers = RANGE * jnp.arange(nbasis, dtype=jnp.float32) / (nbasis - 1)
    sharp = ((nbasis - 1) / RANGE) ** 2
    offset = flat[None, :] - centers[:, None]
    basis = jnp.exp(-sharp * offset * offset)
    pair_in = (proj_a.astype(jnp.float32)[:, :, None] + proj_b.astype(jnp.float32)[:, None, :]).reshape(hidden, -1)
    pre1 = jnp.dot(w_radial, basis, precision=lax.Precision.HIGHEST) + pair_in
    act1 = jax.nn.silu(pre1).astype(jnp.bfloat16)
    pre2 = jnp.dot(w_hidden, act1, preferred_element_type=jnp.float32)
    act2 = jax.nn.silu(pre2).astype(jnp.bfloat16)
    energy = jnp.dot(w_out[None, :], act2, preferred_element_type=jnp.float32)[0]
    back2 = (w_out.astype(jnp.float32)[:, None] * dsilu(pre2)).astype(jnp.bfloat16)
    back1 = lax.dot_general(w_hidden, back2, (((0,), (0,)), ((), ())), preferred_element_type=jnp.float32) * dsilu(pre1)
    radial = lax.dot_general(w_radial, back1, (((0,), (0,)), ((), ())), precision=lax.Precision.HIGHEST)
    slope = lax.optimization_barrier(jnp.sum(radial * basis * (-2.0 * sharp * offset), 0))
    weight = mask * slope.reshape(slots, slots) / dist
    energy_left = lax.optimization_barrier(jnp.sum(mask * energy.reshape(slots, slots), 1))
    pos_left = left[:3]
    pos_right = right[:3]
    force_left = jnp.dot(pos_right, weight.T, precision=lax.Precision.HIGHEST) - pos_left * lax.optimization_barrier(jnp.sum(weight, 1))[None, :]
    force_right = jnp.dot(pos_left, weight, precision=lax.Precision.HIGHEST) - pos_right * lax.optimization_barrier(jnp.sum(weight, 0))[None, :]
    return (force_left, energy_left, force_right)

def reference(positions, features, fill, tiles, tile_count, w_radial, w_left, w_right, w_hidden, w_out):
    live = (jnp.arange(CL, dtype=jnp.int32)[None, :] < fill[:, None]).astype(jnp.float32).reshape(NB)
    coords = jnp.concatenate([positions, live[None, :]], 0)
    proj_left = lax.dot_general(w_left, features, (((0,), (0,)), ((), ())), preferred_element_type=jnp.float32).astype(jnp.bfloat16)
    proj_right = lax.dot_general(w_right, features, (((0,), (0,)), ((), ())), preferred_element_type=jnp.float32).astype(jnp.bfloat16)

    def step(carry, slot):
        firsts, seconds = carry
        device = slot // MAXT
        row_index = device // N_COL
        col_index = device % N_COL
        first = (row_index * GR + tiles[slot, 0]).astype(jnp.int32)
        other = tiles[slot, 1]
        second = ((other // CPD * N_COL + col_index) * CPD + other % CPD).astype(jnp.int32)
        is_live = slot % MAXT < tile_count[device]

        def work(carry):
            firsts, seconds = carry
            start_a = (first * CL).astype(jnp.int32)
            start_b = (second * CL).astype(jnp.int32)
            left = lax.dynamic_slice_in_dim(coords, start_a, CL, 1)
            right = lax.dynamic_slice_in_dim(coords, start_b, CL, 1)
            part_a = lax.dynamic_slice_in_dim(proj_left, start_a, CL, 1)
            part_b = lax.dynamic_slice_in_dim(proj_right, start_b, CL, 1)
            same = (first == second).astype(jnp.float32)
            force_a, energy_a, force_b = tile_terms(left, right, part_a, part_b, same, jnp.float32(1.0), w_radial, w_hidden, w_out)
            added = jnp.concatenate([force_a, energy_a[None, :]], 0)
            firsts = lax.dynamic_update_slice_in_dim(firsts, lax.dynamic_slice_in_dim(firsts, start_a, CL, 1) + added, start_a, 1)
            seconds = lax.dynamic_update_slice_in_dim(seconds, lax.dynamic_slice_in_dim(seconds, start_b, CL, 1) + force_b, start_b, 1)
            return (firsts, seconds)
        return (lax.cond(is_live, work, lambda carry: carry, (firsts, seconds)), None)
    start = (jnp.zeros((4, NB), jnp.float32), jnp.zeros((3, NB), jnp.float32))
    (firsts, seconds), unused = lax.scan(step, start, jnp.arange(NTILES, dtype=jnp.int32))
    return (firsts[:3] + seconds, firsts[3])
```

```python
import functools
import math

import jax
import jax.numpy as jnp
from jax import lax
from jax.experimental import pallas as pl
from jax.experimental.pallas import tpu as pltpu
from jax.sharding import PartitionSpec as P

CL = 128
SOFT = 0.01
RANGE = 6.0
GROUP = 8
STEP = 16
PICK = 16
SEG = 16
PAIR = 16
WIDTHS = (5, 6, 7, 8)
MESH = pl.DeviceIdType.MESH
F32 = jnp.float32
BF16 = jnp.bfloat16


def peers(nrow, ncol, i, j):
    along_col = [(d, lax.rem(j + d, ncol)) for d in range(1, ncol)]
    along_row = [(d, lax.rem(i + d, nrow)) for d in range(1, nrow)]
    return along_col, along_row


def enter(i, j, along_col, along_row):
    barrier = pltpu.get_barrier_semaphore()
    for _, c in along_col:
        pl.semaphore_signal(barrier, inc=1, device_id=(i, c), device_id_type=MESH)
    for _, r in along_row:
        pl.semaphore_signal(barrier, inc=1, device_id=(r, j), device_id_type=MESH)
    return barrier, len(along_col) + len(along_row)


def gather_kernel(
    nrow, ncol, inner, pos_ref, feat_ref, fill_ref, wl_ref, wr_ref,
    rowc_ref, rowp_ref, colc_ref, colp_ref, send_sem, recv_sem,
):
    i = lax.axis_index("row")
    j = lax.axis_index("col")
    outer = nrow // inner
    at_out = i // inner
    at_in = i % inner
    cols = [lax.rem(j + d, ncol) for d in range(1, ncol)]
    outs = [lax.rem(at_out + d, outer) * inner + at_in for d in range(1, outer)]
    origins = [lax.rem(at_out + outer - d, outer) * inner + at_in for d in range(1, outer)]
    mates = [at_out * inner + lax.rem(at_in + d, inner) for d in range(1, inner)]
    barrier = pltpu.get_barrier_semaphore()
    for target in [(r, j) for r in outs + mates] + [(i, c) for c in cols]:
        pl.semaphore_signal(barrier, inc=1, device_id=target, device_id_type=MESH)
    beads = pos_ref.shape[1]
    lane = lax.broadcasted_iota(jnp.int32, (1, CL), 1)
    live = jnp.concatenate(
        [(lane < fill_ref[k]).astype(F32) for k in range(beads // CL)], 1
    )
    coords = jnp.concatenate([pos_ref[...], live], 0)
    rowc_ref[j] = coords
    colc_ref[i] = coords
    dims = (((1,), (0,)), ((), ()))
    feats = feat_ref[...]
    rowp_ref[j] = lax.dot_general(wl_ref[...], feats, dims, preferred_element_type=F32).astype(BF16)
    colp_ref[i] = lax.dot_general(wr_ref[...], feats, dims, preferred_element_type=F32).astype(BF16)
    pl.semaphore_wait(barrier, len(outs) + len(mates) + len(cols))
    started = []

    def send(refs, slot, target):
        copies = []
        for ref in refs:
            k = len(started)
            copy = pltpu.make_async_remote_copy(
                src_ref=ref.at[slot], dst_ref=ref.at[slot],
                send_sem=send_sem.at[k], recv_sem=recv_sem.at[k],
                device_id=target, device_id_type=MESH,
            )
            copy.start()
            started.append(copy)
            copies.append(copy)
        return copies

    late = []
    hops = [send((colp_ref, colc_ref), i, (r, j)) for r in outs]
    for r in mates:
        late += send((colp_ref, colc_ref), i, (r, j))
    for c in cols:
        late += send((rowp_ref, rowc_ref), j, (i, c))
    for copies, origin in zip(hops, origins):
        for copy in copies:
            copy.wait_recv()
        for r in mates:
            late += send((colp_ref, colc_ref), origin, (r, j))
    for copies in hops:
        for copy in copies:
            copy.wait_send()
    for copy in late:
        copy.wait()


def scatter_kernel(
    nrow, ncol, first_ref, second_ref, force_ref, energy_ref, row_in, col_in, send_sem, recv_sem
):
    i = lax.axis_index("row")
    j = lax.axis_index("col")
    along_col, along_row = peers(nrow, ncol, i, j)
    barrier, count = enter(i, j, along_col, along_row)
    pl.semaphore_wait(barrier, count)
    started = []
    for d, r in along_row:
        started.append((second_ref.at[r], col_in.at[d], (r, j)))
    for d, c in along_col:
        started.append((first_ref.at[c], row_in.at[d], (i, c)))
    copies = []
    for k, (src, dst, target) in enumerate(started):
        copy = pltpu.make_async_remote_copy(
            src_ref=src, dst_ref=dst, send_sem=send_sem.at[k], recv_sem=recv_sem.at[k],
            device_id=target, device_id_type=MESH,
        )
        copy.start()
        copies.append(copy)
    total = first_ref[j]
    other = second_ref[i]
    for copy in copies:
        copy.wait()
    for d in range(1, ncol):
        total = total + row_in[d]
    for d in range(1, nrow):
        other = other + col_in[d]
    force_ref[...] = total[:3] + other[:3]
    energy_ref[...] = total[3:4]


def tile_kernel(
    cpd, ncol, tiles_ref, count_ref, rowc_ref, rowp_ref, colc_ref, colp_ref,
    wrad_ref, whid_ref, wout_ref, first_ref, second_ref,
    acc_ref, dist_ref, pack_ref, phi_ref, slope_ref, nphi_ref, nslope_ref,
    proj_ref, pair_src, pair_ref, base_ref, wout_ref8, cent_ref, pick_ref,
):
    row = lax.axis_index("row")
    col = lax.axis_index("col")
    nbasis, hidden = wrad_ref.shape
    clusters = acc_ref.shape[0]
    spacing = RANGE / (nbasis - 1)
    scale = math.sqrt(math.log2(math.e))
    back = -2.0 / (spacing * scale)
    live_count = count_ref[0]
    acc_ref[...] = jnp.zeros_like(acc_ref)
    second_ref[...] = jnp.zeros_like(second_ref)

    depth = 2 * nbasis + PICK
    wide = 0.5 * wrad_ref[...].T
    coarse = wide.astype(BF16).astype(F32)
    base_ref[...] = jnp.concatenate(
        [coarse, jnp.zeros((hidden, PICK), F32), wide - coarse,
         jnp.zeros((hidden, CL - depth), F32)], 1
    )
    whid = whid_ref[...] * jnp.asarray(0.5, BF16)
    wout = jnp.broadcast_to(wout_ref[...].astype(F32), (8, hidden)).T
    wout_ref8[...] = jnp.broadcast_to(wout[:, 0:1], (hidden, CL))
    cent_ref[...] = lax.broadcasted_iota(jnp.int32, (nbasis, CL), 0).astype(F32) * scale
    lanes64 = lax.broadcasted_iota(jnp.int32, (hidden, CL), 1)
    inside = jnp.logical_and(lanes64 >= nbasis, lanes64 < nbasis + PICK)
    segs64 = lanes64 // SEG
    segs = lax.broadcasted_iota(jnp.int32, (CL // 8, CL), 1) // SEG
    lanes = lax.broadcasted_iota(jnp.int32, (CL, CL), 1)
    ident = (lax.broadcasted_iota(jnp.int32, (CL, CL), 0) == lanes).astype(F32)
    pick = lax.broadcasted_iota(jnp.int32, (PICK, 2 * CL), 0)
    pick_lane = lax.broadcasted_iota(jnp.int32, (PICK, 2 * CL), 1)
    for used in WIDTHS:
        for a in range(STEP):
            if a % 8 < used:
                source = jnp.where(pick_lane < used * SEG, a % 8, pick_lane // SEG) + a // 8 * 8
                hit = jnp.logical_and(pick == source, pick_lane < CL)
                pick_ref[used - WIDTHS[0], a] = jnp.where(hit, 1.0, 0.0).astype(BF16)

    def shift(value, amount):
        amount = amount % CL
        return pltpu.roll(value, amount, 1) if amount else value

    @pl.loop(0, live_count)
    def _(slot):
        first = tiles_ref[0, slot]
        other = tiles_ref[1, slot]
        col_a = first // cpd
        row_b = other // cpd
        at_a = pl.ds(pl.multiple_of(first % cpd * CL, CL), CL)
        at_b = pl.ds(pl.multiple_of(other % cpd * CL, CL), CL)
        same = jnp.logical_and(
            jnp.logical_and(col_a == col, row_b == row), first % cpd == other % cpd
        ).astype(F32)
        left = rowc_ref[col_a, :, at_a]
        mine = jnp.concatenate([left, left], 0).T
        proj_ref[...] = 0.5 * rowp_ref[col_a, :, at_a].astype(F32)
        right = colc_ref[row_b, :, at_b]
        pair_src[...] = 0.5 * colp_ref[row_b, :, at_b].astype(F32)
        beads = jnp.sum(left[3:4]).astype(jnp.int32)
        chunks = (beads + STEP - 1) // STEP
        across = jnp.sum(right[3:4]).astype(jnp.int32)
        width = jnp.maximum((across + SEG - 1) // SEG, WIDTHS[0])
        dx = mine[:, 0:1] - right[0:1]
        dy = mine[:, 1:2] - right[1:2]
        dz = mine[:, 2:3] - right[2:3]
        dist = jnp.sqrt(dx * dx + dy * dy + dz * dz + SOFT)
        dist_ref[...] = dist * (scale / spacing)

        def enter(start, used, lhs, half, a):
            scaled = pack_ref[pl.ds(start + (half + a), 1), :]
            off = scaled - cent_ref[...]
            basis = jnp.exp2(-(off * off))
            lift = basis * off
            bump = jnp.concatenate([basis, lift], 1).astype(BF16)
            x1 = jnp.concatenate([bump, pick_ref[used - WIDTHS[0], half + a], bump], 0)
            y1 = jnp.dot(lhs, x1, preferred_element_type=F32)
            h = y1[:, :CL] + pair_ref[a if used < 8 else 0]
            t = jnp.tanh(h)
            u = 1.0 + t
            s = h * u
            d = (u + (1.0 - t) * s) * y1[:, CL:]
            return jnp.concatenate([s, d], 1).astype(BF16)

        def leave(start, half, a, y2):
            h = y2[:, :CL]
            t = jnp.tanh(h)
            u = (1.0 + t) * wout_ref8[...]
            s = h * u
            g = (u + (1.0 - t) * s) * y2[:, CL:]
            spot = pl.ds(pl.multiple_of(start * 8, 8) + (half + a) * 8, 8)
            phi_ref[spot, :] = jnp.sum(s.reshape(hidden // 8, 8, CL), 0)
            slope_ref[spot, :] = jnp.sum(g.reshape(hidden // 8, 8, CL), 0)

        def step(start, used):
            rolled = pltpu.roll(proj_ref[...], lax.rem(nbasis - start + CL, CL), 1)
            lhs = jnp.where(inside, rolled, base_ref[...])[:, :depth].astype(BF16)
            batch = [(half, a) for half in range(0, STEP, GROUP) for a in range(used)]
            for at in range(0, len(batch), PAIR):
                todo = batch[at : at + PAIR]
                hidden_in = [enter(start, used, lhs, half, a) for half, a in todo]
                hidden_out = [jnp.dot(whid, x2, preferred_element_type=F32) for x2 in hidden_in]
                for (half, a), y2 in zip(todo, hidden_out):
                    leave(start, half, a, y2)

        def sweep(used):
            if used == 8:
                pack_ref[...] = dist_ref[...]
                pair_ref[0] = pair_src[...]
            else:
                pair = pair_src[...]
                tails = [dist_ref[pl.ds(k, CL // 8, stride=8), :] for k in range(used, 8)]
                for g in range(used):
                    packed = dist_ref[pl.ds(g, CL // 8, stride=8), :]
                    paired = pair
                    for k in range(used, 8):
                        moved = shift(tails[k - used], SEG * (k - g))
                        packed = jnp.where(segs == k, moved, packed)
                        paired = jnp.where(segs64 == k, shift(pair, SEG * (k - g)), paired)
                    pack_ref[pl.ds(g, CL // 8, stride=8), :] = packed
                    pair_ref[g] = paired

            @pl.loop(0, chunks // 4)
            def _(c):
                start = pl.multiple_of(c * (4 * STEP), 4 * STEP)
                for k in range(4):
                    step(start + k * STEP, used)

            done = chunks // 4 * 4

            @pl.when(chunks % 4 >= 2)
            def _():
                start = pl.multiple_of(done * STEP, 4 * STEP)
                step(start, used)
                step(start + STEP, used)

            @pl.when(chunks % 2 == 1)
            def _():
                step(pl.multiple_of((chunks - 1) * STEP, STEP), used)

            for thin_ref, wide_ref in ((nphi_ref, phi_ref), (nslope_ref, slope_ref)):
                total = wide_ref[pl.ds(0, CL, stride=8), :]
                for k in range(1, 8):
                    total = total + wide_ref[pl.ds(k, CL, stride=8), :]
                thin_ref[...] = total
                if used < 8:
                    parts = [thin_ref[pl.ds(g, CL // 8, stride=8), :] for g in range(used)]
                    for k in range(used, 8):
                        tail = shift(parts[0], -SEG * k)
                        for g in range(1, used):
                            tail = jnp.where(segs == g, shift(parts[g], SEG * (g - k)), tail)
                        thin_ref[pl.ds(k, CL // 8, stride=8), :] = tail

        for used in WIDTHS:
            pl.when(width == used)(functools.partial(sweep, used))

        slope = nslope_ref[...]
        phi = nphi_ref[...]
        both = jnp.logical_and(mine[:, 3:4] * right[3:4] > 0.5, same * ident < 0.5)
        weight = jnp.where(both, back * slope / dist, 0.0)
        phi = jnp.where(both, phi, 0.0)
        wx = weight * dx
        wy = weight * dy
        wz = weight * dz
        energy = jnp.sum(phi, 1, keepdims=True)
        fx = -jnp.sum(wx, 1, keepdims=True)
        fy = -jnp.sum(wy, 1, keepdims=True)
        fz = -jnp.sum(wz, 1, keepdims=True)
        acc_ref[first] = acc_ref[first] + jnp.where(
            lanes == 0, fx, jnp.where(lanes == 1, fy, jnp.where(lanes == 2, fz, energy))
        )
        for k, part in enumerate((wx, wy, wz)):
            total = jnp.sum(part, 0, keepdims=True)
            second_ref[row_b, k : k + 1, at_b] = second_ref[row_b, k : k + 1, at_b] + total

    for k in range(clusters):
        place = (k // cpd, slice(None), slice(k % cpd * CL, k % cpd * CL + CL))
        first_ref[place] = acc_ref[k][:, :8].T


def body(nrow, ncol, positions, features, fill, tiles, tile_count, w_radial, w_left, w_right, w_hidden, w_out):
    beads = positions.shape[1]
    hidden = w_radial.shape[0]
    cpd = fill.shape[0]
    vmem = pl.BlockSpec(memory_space=pltpu.VMEM)
    smem = pl.BlockSpec(memory_space=pltpu.SMEM)
    sends = nrow + ncol - 2
    inner = 2 if nrow % 2 == 0 else 1
    gathered = pl.pallas_call(
        functools.partial(gather_kernel, nrow, ncol, inner),
        name="gather",
        out_shape=(
            jax.ShapeDtypeStruct((ncol, 4, beads), F32),
            jax.ShapeDtypeStruct((ncol, hidden, beads), BF16),
            jax.ShapeDtypeStruct((nrow, 4, beads), F32),
            jax.ShapeDtypeStruct((nrow, hidden, beads), BF16),
        ),
        in_specs=[vmem, vmem, smem, vmem, vmem],
        out_specs=(vmem,) * 4,
        scratch_shapes=[
            pltpu.SemaphoreType.DMA((2 * sends,)),
            pltpu.SemaphoreType.DMA((2 * sends,)),
        ],
        compiler_params=pltpu.CompilerParams(collective_id=0, has_side_effects=True),
    )(positions, features, fill, w_left.T, w_right.T)
    firsts, seconds = pl.pallas_call(
        functools.partial(tile_kernel, cpd, ncol),
        name="tiles",
        out_shape=(
            jax.ShapeDtypeStruct((ncol, 8, beads), F32),
            jax.ShapeDtypeStruct((nrow, 8, beads), F32),
        ),
        in_specs=[smem, smem] + [vmem] * 7,
        out_specs=(vmem, vmem),
        scratch_shapes=[
            pltpu.VMEM((ncol * cpd, CL, CL), F32),
            pltpu.VMEM((CL, CL), F32),
            pltpu.VMEM((CL, CL), F32),
            pltpu.VMEM((CL * 8, CL), F32),
            pltpu.VMEM((CL * 8, CL), F32),
            pltpu.VMEM((CL, CL), F32),
            pltpu.VMEM((CL, CL), F32),
            pltpu.VMEM((hidden, CL), F32),
            pltpu.VMEM((hidden, CL), F32),
            pltpu.VMEM((8, hidden, CL), F32),
            pltpu.VMEM((hidden, CL), F32),
            pltpu.VMEM((hidden, CL), F32),
            pltpu.VMEM((w_radial.shape[1], CL), F32),
            pltpu.VMEM((len(WIDTHS), STEP, PICK, 2 * CL), BF16),
        ],
    )(tiles.T, tile_count, *gathered, w_radial.T, w_hidden, w_out[None, :])
    forces, energy = pl.pallas_call(
        functools.partial(scatter_kernel, nrow, ncol),
        name="scatter",
        out_shape=(
            jax.ShapeDtypeStruct((3, beads), F32),
            jax.ShapeDtypeStruct((1, beads), F32),
        ),
        in_specs=[vmem, vmem],
        out_specs=(vmem, vmem),
        scratch_shapes=[
            pltpu.VMEM((ncol, 8, beads), F32),
            pltpu.VMEM((nrow, 8, beads), F32),
            pltpu.SemaphoreType.DMA((sends,)),
            pltpu.SemaphoreType.DMA((sends,)),
        ],
        compiler_params=pltpu.CompilerParams(collective_id=1, has_side_effects=True),
    )(firsts, seconds)
    return forces, energy[0]


def solution(mesh):
    nrow, ncol = mesh.shape["row"], mesh.shape["col"]
    return jax.shard_map(
        functools.partial(body, nrow, ncol),
        mesh=mesh,
        in_specs=(
            P(None, ("row", "col")),
            P(None, ("row", "col")),
            P(("row", "col")),
            P(("row", "col"), None),
            P(("row", "col")),
            P(),
            P(),
            P(),
            P(),
            P(),
        ),
        out_specs=(P(None, ("row", "col")), P(("row", "col"))),
        check_vma=False,
    )
```

```python
import functools
import math

import jax
import jax.numpy as jnp
from jax import lax
from jax.experimental import pallas as pl
from jax.experimental.pallas import tpu as pltpu
from jax.sharding import PartitionSpec as P

CL = 128
SOFT = 0.01
RANGE = 6.0
STEP = 16
PICK = 16
SEG = 16
LEAST = 4
UNITS = 8
MESH = pl.DeviceIdType.MESH
F32 = jnp.float32
BF16 = jnp.bfloat16


def peers(nrow, ncol, i, j):
    along_col = [(d, lax.rem(j + d, ncol)) for d in range(1, ncol)]
    along_row = [(d, lax.rem(i + d, nrow)) for d in range(1, nrow)]
    return along_col, along_row


def enter(i, j, along_col, along_row):
    barrier = pltpu.get_barrier_semaphore()
    for _, c in along_col:
        pl.semaphore_signal(barrier, inc=1, device_id=(i, c), device_id_type=MESH)
    for _, r in along_row:
        pl.semaphore_signal(barrier, inc=1, device_id=(r, j), device_id_type=MESH)
    return barrier, len(along_col) + len(along_row)


def gather_kernel(
    nrow, ncol, inner, pos_ref, feat_ref, fill_ref, wl_ref, wr_ref,
    rowc_ref, rowp_ref, colc_ref, colp_ref, send_sem, recv_sem,
):
    i = lax.axis_index("row")
    j = lax.axis_index("col")
    outer = nrow // inner
    at_out = i // inner
    at_in = i % inner
    cols = [lax.rem(j + d, ncol) for d in range(1, ncol)]
    outs = [lax.rem(at_out + d, outer) * inner + at_in for d in range(1, outer)]
    origins = [lax.rem(at_out + outer - d, outer) * inner + at_in for d in range(1, outer)]
    mates = [at_out * inner + lax.rem(at_in + d, inner) for d in range(1, inner)]
    barrier = pltpu.get_barrier_semaphore()
    for target in [(r, j) for r in outs + mates] + [(i, c) for c in cols]:
        pl.semaphore_signal(barrier, inc=1, device_id=target, device_id_type=MESH)
    beads = pos_ref.shape[1]
    lane = lax.broadcasted_iota(jnp.int32, (1, CL), 1)
    live = jnp.concatenate(
        [(lane < fill_ref[k]).astype(F32) for k in range(beads // CL)], 1
    )
    coords = jnp.concatenate([pos_ref[...], live], 0)
    rowc_ref[j] = coords
    colc_ref[i] = coords
    dims = (((1,), (0,)), ((), ()))
    feats = feat_ref[...]
    rowp_ref[j] = lax.dot_general(wl_ref[...], feats, dims, preferred_element_type=F32).astype(BF16)
    colp_ref[i] = lax.dot_general(wr_ref[...], feats, dims, preferred_element_type=F32).astype(BF16)
    pl.semaphore_wait(barrier, len(outs) + len(mates) + len(cols))
    started = []

    def send(refs, slot, target):
        copies = []
        for ref in refs:
            k = len(started)
            copy = pltpu.make_async_remote_copy(
                src_ref=ref.at[slot], dst_ref=ref.at[slot],
                send_sem=send_sem.at[k], recv_sem=recv_sem.at[k],
                device_id=target, device_id_type=MESH,
            )
            copy.start()
            started.append(copy)
            copies.append(copy)
        return copies

    late = []
    hops = [send((colp_ref, colc_ref), i, (r, j)) for r in outs]
    for r in mates:
        late += send((colp_ref, colc_ref), i, (r, j))
    for c in cols:
        late += send((rowp_ref, rowc_ref), j, (i, c))
    for copies, origin in zip(hops, origins):
        for copy in copies:
            copy.wait_recv()
        for r in mates:
            late += send((colp_ref, colc_ref), origin, (r, j))
    for copies in hops:
        for copy in copies:
            copy.wait_send()
    for copy in late:
        copy.wait()


def scatter_kernel(
    nrow, ncol, first_ref, second_ref, force_ref, energy_ref, row_in, col_in, send_sem, recv_sem
):
    i = lax.axis_index("row")
    j = lax.axis_index("col")
    along_col, along_row = peers(nrow, ncol, i, j)
    barrier, count = enter(i, j, along_col, along_row)
    pl.semaphore_wait(barrier, count)
    started = []
    for d, r in along_row:
        started.append((second_ref.at[r], col_in.at[d], (r, j)))
    for d, c in along_col:
        started.append((first_ref.at[c], row_in.at[d], (i, c)))
    copies = []
    for k, (src, dst, target) in enumerate(started):
        copy = pltpu.make_async_remote_copy(
            src_ref=src, dst_ref=dst, send_sem=send_sem.at[k], recv_sem=recv_sem.at[k],
            device_id=target, device_id_type=MESH,
        )
        copy.start()
        copies.append(copy)
    total = first_ref[j]
    other = second_ref[i]
    for copy in copies:
        copy.wait()
    for d in range(1, ncol):
        total = total + row_in[d]
    for d in range(1, nrow):
        other = other + col_in[d]
    force_ref[...] = total[:3] + other[:3]
    energy_ref[...] = total[3:4]


def tile_kernel(
    cpd, ncol, tiles_ref, count_ref, rowc_ref, rowp_ref, colc_ref, colp_ref,
    wrad_ref, whid_ref, wout_ref, first_ref, second_ref,
    acc_ref, dist_ref, pack_ref, phi_ref, slope_ref, nphi_ref, nslope_ref,
    proj_ref, pair_src, pair_ref, base_ref, wout_ref8, cent_ref, lhs_ref, pick_ref,
):
    row = lax.axis_index("row")
    col = lax.axis_index("col")
    nbasis, hidden = wrad_ref.shape
    clusters = acc_ref.shape[0]
    spacing = RANGE / (nbasis - 1)
    scale = math.sqrt(math.log2(math.e))
    back = -2.0 / (spacing * scale)
    live_count = count_ref[0]
    acc_ref[...] = jnp.zeros_like(acc_ref)
    second_ref[...] = jnp.zeros_like(second_ref)

    depth = 2 * nbasis + PICK
    wide = 0.5 * wrad_ref[...].T
    coarse = wide.astype(BF16).astype(F32)
    base_ref[...] = jnp.concatenate(
        [coarse, jnp.zeros((hidden, PICK), F32), wide - coarse,
         jnp.zeros((hidden, CL - depth), F32)], 1
    )
    whid = whid_ref[...] * jnp.asarray(0.5, BF16)
    wout = jnp.broadcast_to(wout_ref[...].astype(F32), (8, hidden)).T
    wout_ref8[...] = jnp.broadcast_to(wout[:, 0:1], (hidden, CL))
    cent_ref[...] = lax.broadcasted_iota(jnp.int32, (nbasis, CL), 0).astype(F32) * scale
    lanes64 = lax.broadcasted_iota(jnp.int32, (hidden, CL), 1)
    inside = jnp.logical_and(lanes64 >= nbasis, lanes64 < nbasis + PICK)
    segs64 = lanes64 // SEG
    segs = lax.broadcasted_iota(jnp.int32, (CL // 8, CL), 1) // SEG
    lanes = lax.broadcasted_iota(jnp.int32, (CL, CL), 1)
    ident = (lax.broadcasted_iota(jnp.int32, (CL, CL), 0) == lanes).astype(F32)
    pick = lax.broadcasted_iota(jnp.int32, (PICK, CL), 0)
    pick_seg = lax.broadcasted_iota(jnp.int32, (PICK, CL), 1) // SEG
    pick_ref[...] = jnp.zeros_like(pick_ref)

    def shift(value, amount):
        amount = amount % CL
        return pltpu.roll(value, amount, 1) if amount else value

    @pl.loop(0, live_count)
    def _(slot):
        first = tiles_ref[0, slot]
        other = tiles_ref[1, slot]
        col_a = first // cpd
        row_b = other // cpd
        at_a = pl.ds(pl.multiple_of(first % cpd * CL, CL), CL)
        at_b = pl.ds(pl.multiple_of(other % cpd * CL, CL), CL)
        same = jnp.logical_and(
            jnp.logical_and(col_a == col, row_b == row), first % cpd == other % cpd
        ).astype(F32)
        left = rowc_ref[col_a, :, at_a]
        mine = jnp.concatenate([left, left], 0).T
        proj_ref[...] = 0.5 * rowp_ref[col_a, :, at_a].astype(F32)
        right = colc_ref[row_b, :, at_b]
        pair_src[...] = 0.5 * colp_ref[row_b, :, at_b].astype(F32)
        beads = jnp.sum(left[3:4]).astype(jnp.int32)
        chunks = (beads + STEP - 1) // STEP
        across = jnp.sum(right[3:4]).astype(jnp.int32)
        width = jnp.maximum((across + SEG - 1) // SEG, LEAST)
        dx = mine[:, 0:1] - right[0:1]
        dy = mine[:, 1:2] - right[1:2]
        dz = mine[:, 2:3] - right[2:3]
        dist = jnp.sqrt(dx * dx + dy * dy + dz * dz + SOFT)
        dist_ref[...] = dist * (scale / spacing)

        for g in range(8):
            source = jnp.where(pick_seg < width, g, pick_seg)
            for p in range(2):
                pick_ref[2 * g + p, :, :CL] = jnp.where(pick == source + 8 * p, 1.0, 0.0).astype(BF16)
        for c in range(CL // STEP):
            rolled = shift(proj_ref[...], nbasis - STEP * c)
            lhs_ref[c] = jnp.where(inside, rolled, base_ref[...]).astype(BF16)
        spare = segs >= width
        spare64 = segs64 >= width
        tails = [dist_ref[pl.ds(k, CL // 8, stride=8), :] for k in range(LEAST, 8)]
        for g in range(8):
            moved = shift(tails[0], SEG * (LEAST - g))
            for k in range(LEAST + 1, 8):
                moved = jnp.where(segs >= k, shift(tails[k - LEAST], SEG * (k - g)), moved)
            packed = dist_ref[pl.ds(g, CL // 8, stride=8), :]
            pack_ref[pl.ds(g, CL // 8, stride=8), :] = jnp.where(spare, moved, packed)
        for at in range(0, hidden, 8):
            part = pair_src[at : at + 8, :]
            turned = {j: shift(part, SEG * j) for j in range(LEAST - 7, 8)}
            for g in range(8):
                moved = turned[LEAST - g]
                for k in range(LEAST + 1, 8):
                    moved = jnp.where(segs[:8] >= k, turned[k - g], moved)
                pair_ref[g, at : at + 8, :] = jnp.where(spare64[:8], moved, part)

        def enter(c, g, p):
            off = pack_ref[pl.ds(c * STEP + p * 8 + g, 1), :] - cent_ref[...]
            basis = jnp.exp2(-(off * off))
            lift = basis * off
            bump = jnp.concatenate([basis, lift], 1).astype(BF16)
            x1 = jnp.concatenate([bump, pick_ref[2 * g + p], bump], 0)
            y1 = jnp.dot(lhs_ref[c, :, :depth], x1, preferred_element_type=F32)
            h = y1[:, :CL] + pair_ref[g]
            t = jnp.tanh(h)
            u = 1.0 + t
            s = h * u
            d = (u + (1.0 - t) * s) * y1[:, CL:]
            return jnp.concatenate([s, d], 1).astype(BF16)

        def leave(c, g, p, y2):
            h = y2[:, :CL]
            t = jnp.tanh(h)
            u = (1.0 + t) * wout_ref8[...]
            s = h * u
            d = (u + (1.0 - t) * s) * y2[:, CL:]
            spot = pl.ds(pl.multiple_of((c * STEP + p * 8 + g) * 8, 8), 8)
            phi_ref[spot, :] = jnp.sum(s.reshape(hidden // 8, 8, CL), 0)
            slope_ref[spot, :] = jnp.sum(d.reshape(hidden // 8, 8, CL), 0)

        def block(units, place):
            c, g = place
            for at in range(0, units, UNITS):
                todo = []
                for _ in range(min(UNITS, units)):
                    for p in range(2):
                        todo.append((jnp.minimum(c, CL // STEP - 1), g, p))
                    wrap = g + 1 == width
                    c = c + jnp.where(wrap, 1, 0)
                    g = jnp.where(wrap, 0, g + 1)
                inner = [enter(*row) for row in todo]
                outer = [jnp.dot(whid, x2, preferred_element_type=F32) for x2 in inner]
                for row, y2 in zip(todo, outer):
                    leave(*row, y2)
            return c, g

        count = chunks * width
        large = (count + UNITS - 1) // (2 * UNITS)
        origin = (jnp.int32(0), jnp.int32(0))
        place = lax.fori_loop(0, large, lambda _, at: block(2 * UNITS, at), origin)

        @pl.when(count > large * 2 * UNITS)
        def _():
            block(UNITS, place)

        for thin_ref, wide_ref in ((nphi_ref, phi_ref), (nslope_ref, slope_ref)):
            total = wide_ref[pl.ds(0, CL, stride=8), :]
            for k in range(1, 8):
                total = total + wide_ref[pl.ds(k, CL, stride=8), :]
            thin_ref[...] = total
            parts = [thin_ref[pl.ds(g, CL // 8, stride=8), :] for g in range(8)]
            for k in range(LEAST, 8):
                tail = shift(parts[0], -SEG * k)
                for g in range(1, 7):
                    tail = jnp.where(segs == g, shift(parts[g], SEG * (g - k)), tail)
                thin_ref[pl.ds(k, CL // 8, stride=8), :] = jnp.where(width > k, parts[k], tail)

        slope = nslope_ref[...]
        phi = nphi_ref[...]
        both = jnp.logical_and(mine[:, 3:4] * right[3:4] > 0.5, same * ident < 0.5)
        weight = jnp.where(both, back * slope / dist, 0.0)
        phi = jnp.where(both, phi, 0.0)
        wx = weight * dx
        wy = weight * dy
        wz = weight * dz
        energy = jnp.sum(phi, 1, keepdims=True)
        fx = -jnp.sum(wx, 1, keepdims=True)
        fy = -jnp.sum(wy, 1, keepdims=True)
        fz = -jnp.sum(wz, 1, keepdims=True)
        acc_ref[first] = acc_ref[first] + jnp.where(
            lanes == 0, fx, jnp.where(lanes == 1, fy, jnp.where(lanes == 2, fz, energy))
        )
        for k, part in enumerate((wx, wy, wz)):
            total = jnp.sum(part, 0, keepdims=True)
            second_ref[row_b, k : k + 1, at_b] = second_ref[row_b, k : k + 1, at_b] + total

    for k in range(clusters):
        place = (k // cpd, slice(None), slice(k % cpd * CL, k % cpd * CL + CL))
        first_ref[place] = acc_ref[k][:, :8].T


def body(nrow, ncol, positions, features, fill, tiles, tile_count, w_radial, w_left, w_right, w_hidden, w_out):
    beads = positions.shape[1]
    hidden = w_radial.shape[0]
    cpd = fill.shape[0]
    vmem = pl.BlockSpec(memory_space=pltpu.VMEM)
    smem = pl.BlockSpec(memory_space=pltpu.SMEM)
    sends = nrow + ncol - 2
    inner = 2 if nrow % 2 == 0 else 1
    gathered = pl.pallas_call(
        functools.partial(gather_kernel, nrow, ncol, inner),
        name="gather",
        out_shape=(
            jax.ShapeDtypeStruct((ncol, 4, beads), F32),
            jax.ShapeDtypeStruct((ncol, hidden, beads), BF16),
            jax.ShapeDtypeStruct((nrow, 4, beads), F32),
            jax.ShapeDtypeStruct((nrow, hidden, beads), BF16),
        ),
        in_specs=[vmem, vmem, smem, vmem, vmem],
        out_specs=(vmem,) * 4,
        scratch_shapes=[
            pltpu.SemaphoreType.DMA((2 * sends,)),
            pltpu.SemaphoreType.DMA((2 * sends,)),
        ],
        compiler_params=pltpu.CompilerParams(collective_id=0, has_side_effects=True),
    )(positions, features, fill, w_left.T, w_right.T)
    firsts, seconds = pl.pallas_call(
        functools.partial(tile_kernel, cpd, ncol),
        name="tiles",
        out_shape=(
            jax.ShapeDtypeStruct((ncol, 8, beads), F32),
            jax.ShapeDtypeStruct((nrow, 8, beads), F32),
        ),
        in_specs=[smem, smem] + [vmem] * 7,
        out_specs=(vmem, vmem),
        scratch_shapes=[
            pltpu.VMEM((ncol * cpd, CL, CL), F32),
            pltpu.VMEM((CL, CL), F32),
            pltpu.VMEM((CL, CL), F32),
            pltpu.VMEM((CL * 8, CL), F32),
            pltpu.VMEM((CL * 8, CL), F32),
            pltpu.VMEM((CL, CL), F32),
            pltpu.VMEM((CL, CL), F32),
            pltpu.VMEM((hidden, CL), F32),
            pltpu.VMEM((hidden, CL), F32),
            pltpu.VMEM((8, hidden, CL), F32),
            pltpu.VMEM((hidden, CL), F32),
            pltpu.VMEM((hidden, CL), F32),
            pltpu.VMEM((w_radial.shape[1], CL), F32),
            pltpu.VMEM((CL // STEP, hidden, CL), BF16),
            pltpu.VMEM((16, PICK, 2 * CL), BF16),
        ],
    )(tiles.T, tile_count, *gathered, w_radial.T, w_hidden, w_out[None, :])
    forces, energy = pl.pallas_call(
        functools.partial(scatter_kernel, nrow, ncol),
        name="scatter",
        out_shape=(
            jax.ShapeDtypeStruct((3, beads), F32),
            jax.ShapeDtypeStruct((1, beads), F32),
        ),
        in_specs=[vmem, vmem],
        out_specs=(vmem, vmem),
        scratch_shapes=[
            pltpu.VMEM((ncol, 8, beads), F32),
            pltpu.VMEM((nrow, 8, beads), F32),
            pltpu.SemaphoreType.DMA((sends,)),
            pltpu.SemaphoreType.DMA((sends,)),
        ],
        compiler_params=pltpu.CompilerParams(collective_id=1, has_side_effects=True),
    )(firsts, seconds)
    return forces, energy[0]


def solution(mesh):
    nrow, ncol = mesh.shape["row"], mesh.shape["col"]
    return jax.shard_map(
        functools.partial(body, nrow, ncol),
        mesh=mesh,
        in_specs=(
            P(None, ("row", "col")),
            P(None, ("row", "col")),
            P(("row", "col")),
            P(("row", "col"), None),
            P(("row", "col")),
            P(),
            P(),
            P(),
            P(),
            P(),
        ),
        out_specs=(P(None, ("row", "col")), P(("row", "col"))),
        check_vma=False,
    )
```

```python
import functools
import math

import jax
import jax.numpy as jnp
from jax import lax
from jax.experimental import pallas as pl
from jax.experimental.pallas import tpu as pltpu
from jax.sharding import PartitionSpec as P

CL = 128
SOFT = 0.01
RANGE = 6.0
STEP = 16
PICK = 16
SEG = 16
LEAST = 4
UNITS = 8
MESH = pl.DeviceIdType.MESH
F32 = jnp.float32
BF16 = jnp.bfloat16


def peers(nrow, ncol, i, j):
    along_col = [(d, lax.rem(j + d, ncol)) for d in range(1, ncol)]
    along_row = [(d, lax.rem(i + d, nrow)) for d in range(1, nrow)]
    return along_col, along_row


def enter(i, j, along_col, along_row):
    barrier = pltpu.get_barrier_semaphore()
    for _, c in along_col:
        pl.semaphore_signal(barrier, inc=1, device_id=(i, c), device_id_type=MESH)
    for _, r in along_row:
        pl.semaphore_signal(barrier, inc=1, device_id=(r, j), device_id_type=MESH)
    return barrier, len(along_col) + len(along_row)


def gather_kernel(
    nrow, ncol, inner, pos_ref, feat_ref, fill_ref, wl_ref, wr_ref,
    rowc_ref, rowp_ref, colc_ref, colp_ref, send_sem, recv_sem,
):
    i = lax.axis_index("row")
    j = lax.axis_index("col")
    outer = nrow // inner
    at_out = i // inner
    at_in = i % inner
    cols = [lax.rem(j + d, ncol) for d in range(1, ncol)]
    outs = [lax.rem(at_out + d, outer) * inner + at_in for d in range(1, outer)]
    origins = [lax.rem(at_out + outer - d, outer) * inner + at_in for d in range(1, outer)]
    mates = [at_out * inner + lax.rem(at_in + d, inner) for d in range(1, inner)]
    barrier = pltpu.get_barrier_semaphore()
    for target in [(r, j) for r in outs + mates] + [(i, c) for c in cols]:
        pl.semaphore_signal(barrier, inc=1, device_id=target, device_id_type=MESH)
    beads = pos_ref.shape[1]
    lane = lax.broadcasted_iota(jnp.int32, (1, CL), 1)
    live = jnp.concatenate(
        [(lane < fill_ref[k]).astype(F32) for k in range(beads // CL)], 1
    )
    coords = jnp.concatenate([pos_ref[...], live], 0)
    rowc_ref[j] = coords
    colc_ref[i] = coords
    dims = (((1,), (0,)), ((), ()))
    feats = feat_ref[...]
    rowp_ref[j] = lax.dot_general(wl_ref[...], feats, dims, preferred_element_type=F32).astype(BF16)
    colp_ref[i] = lax.dot_general(wr_ref[...], feats, dims, preferred_element_type=F32).astype(BF16)
    pl.semaphore_wait(barrier, len(outs) + len(mates) + len(cols))
    started = []

    def send(refs, slot, target):
        copies = []
        for ref in refs:
            k = len(started)
            copy = pltpu.make_async_remote_copy(
                src_ref=ref.at[slot], dst_ref=ref.at[slot],
                send_sem=send_sem.at[k], recv_sem=recv_sem.at[k],
                device_id=target, device_id_type=MESH,
            )
            copy.start()
            started.append(copy)
            copies.append(copy)
        return copies

    late = []
    hops = [send((colp_ref, colc_ref), i, (r, j)) for r in outs]
    for r in mates:
        late += send((colp_ref, colc_ref), i, (r, j))
    for c in cols:
        late += send((rowp_ref, rowc_ref), j, (i, c))
    for copies, origin in zip(hops, origins):
        for copy in copies:
            copy.wait_recv()
        for r in mates:
            late += send((colp_ref, colc_ref), origin, (r, j))
    for copies in hops:
        for copy in copies:
            copy.wait_send()
    for copy in late:
        copy.wait()


def scatter_kernel(
    nrow, ncol, first_ref, second_ref, total_ref, other_ref, row_in, col_in, send_sem, recv_sem
):
    i = lax.axis_index("row")
    j = lax.axis_index("col")
    along_col, along_row = peers(nrow, ncol, i, j)
    barrier, count = enter(i, j, along_col, along_row)
    pl.semaphore_wait(barrier, count)
    started = []
    for d, r in along_row:
        started.append((second_ref.at[r], col_in.at[d], (r, j)))
    for d, c in along_col:
        started.append((first_ref.at[c], row_in.at[d], (i, c)))
    copies = []
    for k, (src, dst, target) in enumerate(started):
        copy = pltpu.make_async_remote_copy(
            src_ref=src, dst_ref=dst, send_sem=send_sem.at[k], recv_sem=recv_sem.at[k],
            device_id=target, device_id_type=MESH,
        )
        copy.start()
        copies.append(copy)
    total = first_ref[j]
    other = second_ref[i]
    for copy in copies:
        copy.wait()
    for d in range(1, ncol):
        total = total + row_in[d]
    for d in range(1, nrow):
        other = other + col_in[d]
    total_ref[...] = total[:4]
    other_ref[...] = other[:3]


def tile_kernel(
    cpd, ncol, tiles_ref, count_ref, rowc_ref, rowp_ref, colc_ref, colp_ref,
    wrad_ref, whid_ref, wout_ref, first_ref, second_ref,
    acc_ref, dist_ref, pack_ref, phi_ref, slope_ref, nphi_ref, nslope_ref,
    proj_ref, pair_src, pair_ref, base_ref, wout_ref8, cent_ref, lhs_ref, pick_ref,
):
    row = lax.axis_index("row")
    col = lax.axis_index("col")
    nbasis, hidden = wrad_ref.shape
    clusters = acc_ref.shape[0]
    spacing = RANGE / (nbasis - 1)
    scale = math.sqrt(math.log2(math.e))
    back = -2.0 / (spacing * scale)
    live_count = count_ref[0]
    acc_ref[...] = jnp.zeros_like(acc_ref)
    second_ref[...] = jnp.zeros_like(second_ref)

    depth = 2 * nbasis + PICK
    wide = 0.5 * wrad_ref[...].T
    coarse = wide.astype(BF16).astype(F32)
    base_ref[...] = jnp.concatenate(
        [coarse, jnp.zeros((hidden, PICK), F32), wide - coarse,
         jnp.zeros((hidden, CL - depth), F32)], 1
    )
    whid = whid_ref[...] * jnp.asarray(0.5, BF16)
    wout = jnp.broadcast_to(wout_ref[...].astype(F32), (8, hidden)).T
    wout_ref8[...] = jnp.broadcast_to(wout[:, 0:1], (hidden, CL))
    cent_ref[...] = lax.broadcasted_iota(jnp.int32, (nbasis, CL), 0).astype(F32) * scale
    lanes64 = lax.broadcasted_iota(jnp.int32, (hidden, CL), 1)
    inside = jnp.logical_and(lanes64 >= nbasis, lanes64 < nbasis + PICK)
    segs64 = lanes64 // SEG
    segs = lax.broadcasted_iota(jnp.int32, (CL // 8, CL), 1) // SEG
    lanes = lax.broadcasted_iota(jnp.int32, (CL, CL), 1)
    ident = (lax.broadcasted_iota(jnp.int32, (CL, CL), 0) == lanes).astype(F32)
    pick = lax.broadcasted_iota(jnp.int32, (PICK, CL), 0)
    pick_seg = lax.broadcasted_iota(jnp.int32, (PICK, CL), 1) // SEG
    pick_ref[...] = jnp.zeros_like(pick_ref)

    def shift(value, amount):
        amount = amount % CL
        return pltpu.roll(value, amount, 1) if amount else value

    @pl.loop(0, live_count)
    def _(slot):
        first = tiles_ref[0, slot]
        other = tiles_ref[1, slot]
        col_a = first // cpd
        row_b = other // cpd
        at_a = pl.ds(pl.multiple_of(first % cpd * CL, CL), CL)
        at_b = pl.ds(pl.multiple_of(other % cpd * CL, CL), CL)
        same = jnp.logical_and(
            jnp.logical_and(col_a == col, row_b == row), first % cpd == other % cpd
        ).astype(F32)
        left = rowc_ref[col_a, :, at_a]
        mine = jnp.concatenate([left, left], 0).T
        proj_ref[...] = 0.5 * rowp_ref[col_a, :, at_a].astype(F32)
        right = colc_ref[row_b, :, at_b]
        pair_src[...] = 0.5 * colp_ref[row_b, :, at_b].astype(F32)
        beads = jnp.sum(left[3:4]).astype(jnp.int32)
        chunks = (beads + STEP - 1) // STEP
        across = jnp.sum(right[3:4]).astype(jnp.int32)
        width = jnp.maximum((across + SEG - 1) // SEG, LEAST)
        dx = mine[:, 0:1] - right[0:1]
        dy = mine[:, 1:2] - right[1:2]
        dz = mine[:, 2:3] - right[2:3]
        dist = jnp.sqrt(dx * dx + dy * dy + dz * dz + SOFT)
        dist_ref[...] = dist * (scale / spacing)

        for g in range(8):
            source = jnp.where(pick_seg < width, g, pick_seg)
            for p in range(2):
                pick_ref[2 * g + p, :, :CL] = jnp.where(pick == source + 8 * p, 1.0, 0.0).astype(BF16)
        for c in range(CL // STEP):
            rolled = shift(proj_ref[...], nbasis - STEP * c)
            lhs_ref[c] = jnp.where(inside, rolled, base_ref[...]).astype(BF16)
        spare = segs >= width
        spare64 = segs64 >= width
        tails = [dist_ref[pl.ds(k, CL // 8, stride=8), :] for k in range(LEAST, 8)]
        for g in range(8):
            moved = shift(tails[0], SEG * (LEAST - g))
            for k in range(LEAST + 1, 8):
                moved = jnp.where(segs >= k, shift(tails[k - LEAST], SEG * (k - g)), moved)
            packed = dist_ref[pl.ds(g, CL // 8, stride=8), :]
            pack_ref[pl.ds(g, CL // 8, stride=8), :] = jnp.where(spare, moved, packed)
        for at in range(0, hidden, 8):
            part = pair_src[at : at + 8, :]
            turned = {j: shift(part, SEG * j) for j in range(LEAST - 7, 8)}
            for g in range(8):
                moved = turned[LEAST - g]
                for k in range(LEAST + 1, 8):
                    moved = jnp.where(segs[:8] >= k, turned[k - g], moved)
                pair_ref[g, at : at + 8, :] = jnp.where(spare64[:8], moved, part)

        def enter(c, g, p):
            off = pack_ref[pl.ds(c * STEP + p * 8 + g, 1), :] - cent_ref[...]
            basis = jnp.exp2(-(off * off))
            lift = basis * off
            bump = jnp.concatenate([basis, lift], 1).astype(BF16)
            x1 = jnp.concatenate([bump, pick_ref[2 * g + p], bump], 0)
            y1 = jnp.dot(lhs_ref[c, :, :depth], x1, preferred_element_type=F32)
            h = y1[:, :CL] + pair_ref[g]
            t = jnp.tanh(h)
            u = 1.0 + t
            s = h * u
            d = (u + (1.0 - t) * s) * y1[:, CL:]
            return jnp.concatenate([s, d], 1).astype(BF16)

        def leave(c, g, p, y2):
            h = y2[:, :CL]
            t = jnp.tanh(h)
            u = (1.0 + t) * wout_ref8[...]
            s = h * u
            d = (u + (1.0 - t) * s) * y2[:, CL:]
            spot = pl.ds(pl.multiple_of((c * STEP + p * 8 + g) * 8, 8), 8)
            phi_ref[spot, :] = jnp.sum(s.reshape(hidden // 8, 8, CL), 0)
            slope_ref[spot, :] = jnp.sum(d.reshape(hidden // 8, 8, CL), 0)

        def block(units, place):
            c, g = place
            for at in range(0, units, UNITS):
                todo = []
                for _ in range(min(UNITS, units)):
                    for p in range(2):
                        todo.append((jnp.minimum(c, CL // STEP - 1), g, p))
                    wrap = g + 1 == width
                    c = c + jnp.where(wrap, 1, 0)
                    g = jnp.where(wrap, 0, g + 1)
                inner = [enter(*row) for row in todo]
                outer = [jnp.dot(whid, x2, preferred_element_type=F32) for x2 in inner]
                for row, y2 in zip(todo, outer):
                    leave(*row, y2)
            return c, g

        count = chunks * width
        large = (count + UNITS - 1) // (2 * UNITS)
        origin = (jnp.int32(0), jnp.int32(0))
        place = lax.fori_loop(0, large, lambda _, at: block(2 * UNITS, at), origin)

        @pl.when(count > large * 2 * UNITS)
        def _():
            block(UNITS, place)

        for thin_ref, wide_ref in ((nphi_ref, phi_ref), (nslope_ref, slope_ref)):
            total = wide_ref[pl.ds(0, CL, stride=8), :]
            for k in range(1, 8):
                total = total + wide_ref[pl.ds(k, CL, stride=8), :]
            thin_ref[...] = total
            parts = [thin_ref[pl.ds(g, CL // 8, stride=8), :] for g in range(8)]
            for k in range(LEAST, 8):
                tail = shift(parts[0], -SEG * k)
                for g in range(1, 7):
                    tail = jnp.where(segs == g, shift(parts[g], SEG * (g - k)), tail)
                thin_ref[pl.ds(k, CL // 8, stride=8), :] = jnp.where(width > k, parts[k], tail)

        slope = nslope_ref[...]
        phi = nphi_ref[...]
        both = jnp.logical_and(mine[:, 3:4] * right[3:4] > 0.5, same * ident < 0.5)
        weight = jnp.where(both, back * slope / dist, 0.0)
        phi = jnp.where(both, phi, 0.0)
        wx = weight * dx
        wy = weight * dy
        wz = weight * dz
        energy = jnp.sum(phi, 1, keepdims=True)
        fx = -jnp.sum(wx, 1, keepdims=True)
        fy = -jnp.sum(wy, 1, keepdims=True)
        fz = -jnp.sum(wz, 1, keepdims=True)
        acc_ref[first] = acc_ref[first] + jnp.where(
            lanes == 0, fx, jnp.where(lanes == 1, fy, jnp.where(lanes == 2, fz, energy))
        )
        for k, part in enumerate((wx, wy, wz)):
            total = jnp.sum(part, 0, keepdims=True)
            second_ref[row_b, k : k + 1, at_b] = second_ref[row_b, k : k + 1, at_b] + total

    for k in range(clusters):
        place = (k // cpd, slice(None), slice(k % cpd * CL, k % cpd * CL + CL))
        first_ref[place] = acc_ref[k][:, :8].T


def body(nrow, ncol, positions, features, fill, tiles, tile_count, w_radial, w_left, w_right, w_hidden, w_out):
    beads = positions.shape[1]
    hidden = w_radial.shape[0]
    cpd = fill.shape[0]
    vmem = pl.BlockSpec(memory_space=pltpu.VMEM)
    smem = pl.BlockSpec(memory_space=pltpu.SMEM)
    sends = nrow + ncol - 2
    inner = 2 if nrow % 2 == 0 else 1
    gathered = pl.pallas_call(
        functools.partial(gather_kernel, nrow, ncol, inner),
        name="gather",
        out_shape=(
            jax.ShapeDtypeStruct((ncol, 4, beads), F32),
            jax.ShapeDtypeStruct((ncol, hidden, beads), BF16),
            jax.ShapeDtypeStruct((nrow, 4, beads), F32),
            jax.ShapeDtypeStruct((nrow, hidden, beads), BF16),
        ),
        in_specs=[vmem, vmem, smem, vmem, vmem],
        out_specs=(vmem,) * 4,
        scratch_shapes=[
            pltpu.SemaphoreType.DMA((2 * sends,)),
            pltpu.SemaphoreType.DMA((2 * sends,)),
        ],
        compiler_params=pltpu.CompilerParams(collective_id=0, has_side_effects=True),
    )(positions, features, fill, w_left.T, w_right.T)
    firsts, seconds = pl.pallas_call(
        functools.partial(tile_kernel, cpd, ncol),
        name="tiles",
        out_shape=(
            jax.ShapeDtypeStruct((ncol, 8, beads), F32),
            jax.ShapeDtypeStruct((nrow, 8, beads), F32),
        ),
        in_specs=[smem, smem] + [vmem] * 7,
        out_specs=(vmem, vmem),
        scratch_shapes=[
            pltpu.VMEM((ncol * cpd, CL, CL), F32),
            pltpu.VMEM((CL, CL), F32),
            pltpu.VMEM((CL, CL), F32),
            pltpu.VMEM((CL * 8, CL), F32),
            pltpu.VMEM((CL * 8, CL), F32),
            pltpu.VMEM((CL, CL), F32),
            pltpu.VMEM((CL, CL), F32),
            pltpu.VMEM((hidden, CL), F32),
            pltpu.VMEM((hidden, CL), F32),
            pltpu.VMEM((8, hidden, CL), F32),
            pltpu.VMEM((hidden, CL), F32),
            pltpu.VMEM((hidden, CL), F32),
            pltpu.VMEM((w_radial.shape[1], CL), F32),
            pltpu.VMEM((CL // STEP, hidden, CL), BF16),
            pltpu.VMEM((16, PICK, 2 * CL), BF16),
        ],
    )(tiles.T, tile_count, *gathered, w_radial.T, w_hidden, w_out[None, :])
    total, other = pl.pallas_call(
        functools.partial(scatter_kernel, nrow, ncol),
        name="scatter",
        out_shape=(
            jax.ShapeDtypeStruct((4, beads), F32),
            jax.ShapeDtypeStruct((3, beads), F32),
        ),
        in_specs=[vmem, vmem],
        out_specs=(vmem, vmem),
        scratch_shapes=[
            pltpu.VMEM((ncol, 8, beads), F32),
            pltpu.VMEM((nrow, 8, beads), F32),
            pltpu.SemaphoreType.DMA((sends,)),
            pltpu.SemaphoreType.DMA((sends,)),
        ],
        compiler_params=pltpu.CompilerParams(collective_id=1, has_side_effects=True),
    )(firsts, seconds)
    return total[:3] + other, total[3]


def solution(mesh):
    nrow, ncol = mesh.shape["row"], mesh.shape["col"]
    return jax.shard_map(
        functools.partial(body, nrow, ncol),
        mesh=mesh,
        in_specs=(
            P(None, ("row", "col")),
            P(None, ("row", "col")),
            P(("row", "col")),
            P(("row", "col"), None),
            P(("row", "col")),
            P(),
            P(),
            P(),
            P(),
            P(),
        ),
        out_specs=(P(None, ("row", "col")), P(("row", "col"))),
        check_vma=False,
    )
```
